32 devices in a mesh: ha: 2 (over y), wa: 16 (over z, x, core).
Axes of the slice: x: 2, y: 2, z: 4, core: 2. Of those that a mesh axis runs over, the one named last changes fastest.
Arguments:
- block_input: bfloat16 [3, 46, 160, 128], P(None, 'ha', 'wa'), may hold values from -6 to 6
- cotangent: bfloat16 [3, 46, 160, 128], P(None, 'ha', 'wa'), may hold values from -6 to 6
- kernel_one: bfloat16 [3, 3, 3, 128, 128], replicated, may hold values from -0.109375 to 0.109375
- bias_one: float32 [128], replicated, may hold values from -3 to 3
- kernel_two: bfloat16 [3, 3, 3, 128, 128], replicated, may hold values from -0.109375 to 0.109375
- scale_one: float32 [128], replicated, may hold values from 0.5 to 2
- shift_one: float32 [128], replicated, may hold values from -1 to 1
- scale_two: float32 [128], replicated, may hold values from 0.5 to 2
- shift_two: float32 [128], replicated, may hold values from -1 to 1
Outputs:
- grad_input: bfloat16 [3, 46, 160, 128], P(None, 'ha', 'wa')
- grad_kernel_one: float32 [3, 3, 3, 128, 128], replicated
- grad_bias_one: float32 [128], replicated
- grad_kernel_two: float32 [3, 3, 3, 128, 128], replicated
- grad_bias_two: float32 [128], replicated
The draws below stay inside these ranges and needn't reach their ends.
All inputs are finite; a program needn't handle non-finite values.
Results may differ from the reference program's by a relative error of at most 0.0054.
Values may be sent and summed in bfloat16 or wider, within the bound.
A program may use at most 64 MiB of HBM per device.

```python
import math
import jax
import jax.numpy as jnp
from jax import lax

CHANNELS = 128
FRAMES = 3
HEIGHT = 46
WIDTH = 160
CELLS = 22080


def level_of(stream_key, shape, split, least, largest):
    gain = 1.0
    for dim, parts in split:
        steps = jax.random.uniform(jax.random.fold_in(jax.random.fold_in(stream_key, 6), dim), (parts,), jnp.float32, least / len(split), largest / len(split))
        gain = gain * jnp.repeat(jnp.exp(steps), shape[dim] // parts).reshape((-1,) + (1,) * (len(shape) - 1 - dim))
    return gain


def noise(rng, dims, spread, limit, pieces=(), kind=jnp.bfloat16):
    entries = jax.random.normal(rng, dims, jnp.float32) * spread
    if len(pieces) > 0:
        entries = level_of(rng, dims, pieces, -0.22, 0.18) * entries
    return jnp.clip(entries, min=-limit, max=limit).astype(kind)


def setup_inputs(seed: int = 0) -> dict:
    key_list = jax.random.split(jax.random.key(seed), 10)
    return {
        "block_input": noise(key_list[0], (FRAMES, HEIGHT, WIDTH, CHANNELS), 1.0, 6.0, ((1, 2), (2, 16))),
        "cotangent": noise(key_list[1], (FRAMES, HEIGHT, WIDTH, CHANNELS), 1.0, 6.0, ((1, 2), (2, 16))),
        "kernel_one": noise(key_list[2], (3, 3, 3, CHANNELS, CHANNELS), (27 * CHANNELS) ** -0.5, 0.109375),
        "bias_one": noise(key_list[3], (CHANNELS,), 0.5, 3.0, (), jnp.float32),
        "kernel_two": noise(key_list[4], (3, 3, 3, CHANNELS, CHANNELS), (27 * CHANNELS) ** -0.5, 0.109375),
        "scale_one": jnp.clip(jnp.exp(jax.random.uniform(key_list[5], (CHANNELS,), jnp.float32, math.log(0.5), math.log(2.0))), 0.5, 2.0),
        "shift_one": jnp.clip(jax.random.uniform(key_list[6], (CHANNELS,), jnp.float32, -1.0, 1.0), -1.0, 1.0),
        "scale_two": jnp.clip(jnp.exp(jax.random.uniform(key_list[7], (CHANNELS,), jnp.float32, math.log(0.5), math.log(2.0))), 0.5, 2.0),
        "shift_two": jnp.clip(jax.random.uniform(key_list[8], (CHANNELS,), jnp.float32, -1.0, 1.0), -1.0, 1.0),
    }


def convolve(field, kernel):
    out = lax.conv_general_dilated(field[None], kernel, (1, 1, 1), ((2, 0), (1, 1), (1, 1)), dimension_numbers=('NDHWC', 'DHWIO', 'NDHWC'), precision=lax.Precision.HIGHEST)
    return out[0]

def slope(value):
    sigma = jax.nn.sigmoid(value)
    return sigma * (1.0 + value * (1.0 - sigma))

def reference(block_input, cotangent, kernel_one, bias_one, kernel_two, scale_one, shift_one, scale_two, shift_two):
    factor = 1.0 / math.sqrt(CELLS)
    first_pre = block_input.astype(jnp.float32) * scale_one + shift_one
    first_act = jax.nn.silu(first_pre).astype(jnp.bfloat16)
    first_f = first_act.astype(jnp.float32)
    kernel_a = kernel_one.astype(jnp.float32)
    kernel_b = kernel_two.astype(jnp.float32)
    hidden = convolve(first_f, kernel_a) + bias_one
    second_pre = hidden * scale_two + shift_two
    second_act = jax.nn.silu(second_pre).astype(jnp.bfloat16)
    upstream = cotangent.astype(jnp.float32)
    unused, pull_two = jax.vjp(convolve, second_act.astype(jnp.float32), kernel_b)
    back_two, grad_two = pull_two(upstream)
    inner = (back_two * slope(second_pre) * scale_two).astype(jnp.bfloat16)
    unused, pull_one = jax.vjp(convolve, first_f, kernel_a)
    back_one, grad_one = pull_one(inner.astype(jnp.float32))
    grad_input = (upstream + back_one * slope(first_pre) * scale_one).astype(jnp.bfloat16)
    bias_a = lax.optimization_barrier(jnp.sum(inner.astype(jnp.float32), axis=(0, 1, 2)))
    bias_b = lax.optimization_barrier(jnp.sum(upstream, axis=(0, 1, 2)))
    return (grad_input, grad_one * factor, bias_a * factor, grad_two * factor, bias_b * factor)
```

```python
import functools
import math

import jax
import jax.numpy as jnp
from jax import lax
from jax.experimental import pallas as pl
from jax.experimental.pallas import tpu as pltpu
from jax.sharding import PartitionSpec as P

MESH = pl.DeviceIdType.MESH
F32 = jnp.float32
BF16 = jnp.bfloat16
VMEM = pl.BlockSpec(memory_space=pltpu.VMEM)
DIRECTIONS = [(dy, dx) for dy in (-1, 0, 1) for dx in (-1, 0, 1) if (dy, dx) != (0, 0)]
RIM = 2


def span(step, size):
    return {-1: (0, RIM), 0: (0, size), 1: (size - RIM, size)}[step]


def rim_shape(direction, frames, rows, columns, chans):
    dy, dx = direction
    return (2 * frames, rows if dy == 0 else RIM, columns if dx == 0 else RIM, chans)


def neighbour(direction, me, sizes):
    there = [m + d for m, d in zip(me, direction)]
    exists = True
    for place, size, d in zip(there, sizes, direction):
        if d < 0:
            exists = jnp.logical_and(exists, place >= 0)
        if d > 0:
            exists = jnp.logical_and(exists, place < size)
    return exists, tuple(there)


def halo_kernel(sizes, x_ref, g_ref, *refs):
    recv = refs[:8]
    stage = refs[8:16]
    send_sem, recv_sem = refs[16:]
    frames, rows, columns, _ = x_ref.shape
    me = (lax.axis_index("ha"), lax.axis_index("wa"))
    barrier = pltpu.get_barrier_semaphore()
    places = [neighbour(d, me, sizes) for d in DIRECTIONS]
    for exists, there in places:

        @pl.when(exists)
        def _(there=there):
            pl.semaphore_signal(barrier, inc=1, device_id=there, device_id_type=MESH)

    for which, ref in enumerate((x_ref, g_ref)):
        whole = ref[...].astype(F32)
        for k, (dy, dx) in enumerate(DIRECTIONS):
            r0, r1 = span(dy, rows)
            c0, c1 = span(dx, columns)
            stage[k][which * frames : (which + 1) * frames] = whole[:, r0:r1, c0:c1].astype(BF16)
    pl.semaphore_wait(barrier, sum(jnp.where(exists, 1, 0) for exists, _ in places))
    copies = []
    for k, (exists, there) in enumerate(places):
        opposite = 7 - k
        copy = pltpu.make_async_remote_copy(
            src_ref=stage[k],
            dst_ref=recv[opposite],
            send_sem=send_sem.at[k],
            recv_sem=recv_sem.at[opposite],
            device_id=there,
            device_id_type=MESH,
        )
        pl.when(exists)(copy.start)
        copies.append(copy)
    for k, (exists, there) in enumerate(places):

        @pl.when(exists)
        def _(k=k, there=there):
            copies[k].wait_send()
            pltpu.make_async_remote_copy(
                src_ref=stage[k],
                dst_ref=recv[k],
                send_sem=send_sem.at[k],
                recv_sem=recv_sem.at[k],
                device_id=there,
                device_id_type=MESH,
            ).wait_recv()


def halo(x, g, sizes):
    frames, rows, columns, chans = x.shape
    shapes = [rim_shape(d, frames, rows, columns, chans) for d in DIRECTIONS]
    return pl.pallas_call(
        functools.partial(halo_kernel, sizes),
        name="halo",
        out_shape=[jax.ShapeDtypeStruct(s, BF16) for s in shapes],
        in_specs=[VMEM, VMEM],
        out_specs=[VMEM] * 8,
        scratch_shapes=[pltpu.VMEM(s, BF16) for s in shapes]
        + [pltpu.SemaphoreType.DMA((8,)), pltpu.SemaphoreType.DMA((8,))],
        compiler_params=pltpu.CompilerParams(collective_id=0, has_side_effects=True),
    )(x, g)


def sigmoid(value):
    return 1.0 / (1.0 + jnp.exp(-value))


def store_wide(wide, t, value):
    rows, cols, chans = value.shape
    flat = value.reshape(rows * cols, chans)
    for kw in range(3):
        moved = flat if kw == 0 else pltpu.roll(flat, rows * cols - kw, 0)
        wide[t, :, :, kw * chans : (kw + 1) * chans] = moved.reshape(rows, cols, chans).astype(BF16)


def flat2(value):
    return value.reshape(-1, value.shape[-1])


def dot(a, b, dims):
    return lax.dot_general(a, b, (dims, ((), ())), preferred_element_type=F32)


def compute_kernel(
    sizes,
    x_ref,
    g_ref,
    k1_ref,
    b1_ref,
    k2_ref,
    s1_ref,
    h1_ref,
    s2_ref,
    h2_ref,
    *refs,
):
    recv = refs[:8]
    out_ref, terms = refs[8:10]
    pad, w1, wg, w2, wd, ds2, own = refs[10:]
    frames, rows, columns, chans = x_ref.shape
    deep, cols = pad.shape[2:4]
    inner = rows + 2
    taps = 27 * chans
    me = (lax.axis_index("ha"), lax.axis_index("wa"))

    pad[...] = jnp.zeros_like(pad)
    pad[0, :, RIM : RIM + rows, RIM : RIM + columns] = x_ref[...].astype(F32)
    pad[1, :, RIM : RIM + rows, RIM : RIM + columns] = g_ref[...].astype(F32)
    starts = {-1: 0, 0: RIM}
    for k, direction in enumerate(DIRECTIONS):
        exists, _ = neighbour(direction, me, sizes)
        r0 = starts.get(direction[0], RIM + rows)
        c0 = starts.get(direction[1], RIM + columns)
        _, nr, nc, _ = recv[k].shape

        @pl.when(exists)
        def _(k=k, r0=r0, c0=c0, nr=nr, nc=nc):
            value = recv[k][...].astype(F32)
            for which in range(2):
                pad[which, :, r0 : r0 + nr, c0 : c0 + nc] = value[
                    which * frames : (which + 1) * frames
                ]

    def inside(depth, wide, rim):
        shape = (depth, cols, chans)
        r = lax.broadcasted_iota(jnp.int32, shape, 0) + (me[0] * rows - rim)
        c = lax.broadcasted_iota(jnp.int32, shape, 1)
        place = c + (me[1] * columns - rim)
        ok = (r >= 0) & (r < rows * sizes[0]) & (place >= 0) & (place < columns * sizes[1])
        return ok & (c < wide)

    s1 = s1_ref[...]
    h1 = h1_ref[...]
    s2 = s2_ref[...]
    h2 = h2_ref[...]
    ok1 = inside(deep, columns + 2 * RIM, RIM)
    for t in range(frames):
        z1 = pad[0, t] * s1 + h1
        store_wide(w1, t, jnp.where(ok1, z1 * sigmoid(z1), 0.0))
        store_wide(wg, t, pad[1, t])
        own[0, t] = jnp.zeros_like(own[0, t])
        own[0, t, :, :columns] = g_ref[t].astype(F32)

    ok2 = inside(inner, columns + 2, 1)
    for t in range(frames):
        total = jnp.zeros((inner * cols, chans), F32)
        for kt in range(2 - t, 3) if t < 2 else range(3):
            for kh in range(3):
                total = total + dot(
                    flat2(w1[t + kt - 2, kh : kh + inner]),
                    k1_ref[kt, kh].reshape(3 * chans, chans),
                    ((1,), (0,)),
                )
        z2 = (total.reshape(inner, cols, chans) + b1_ref[...]) * s2 + h2
        sig = sigmoid(z2)
        store_wide(w2, t, jnp.where(ok2, z2 * sig, 0.0))
        ds2[t] = jnp.where(ok2, sig * (1.0 + z2 * (1.0 - sig)) * s2, 0.0)

    gown = own[0].astype(BF16)
    for kt in range(3):
        for kh in range(3):
            first = 2 - kt
            slab = w2[: frames - first, kh : kh + rows]
            term = dot(flat2(slab), flat2(gown[first:]), ((0,), (0,)))
            terms[0, (kt * 3 + kh) * 3 * chans : (kt * 3 + kh + 1) * 3 * chans] = term

    def back(wide, kernel_ref, t, depth):
        total = jnp.zeros((depth * cols, chans), F32)
        for kt in range(t, 3):
            for kh in range(3):
                weights = jnp.concatenate(
                    [kernel_ref[kt, 2 - kh, 2 - kw] for kw in range(3)], axis=1
                )
                total = total + dot(
                    flat2(wide[t + 2 - kt, kh : kh + depth]), weights, ((1,), (1,))
                )
        return total.reshape(depth, cols, chans)

    c = lax.broadcasted_iota(jnp.int32, (rows, cols, chans), 1)
    mine = (c >= 1) & (c <= columns)
    bias = [jnp.zeros((1, chans), F32), jnp.zeros((1, chans), F32)]
    for t in range(frames):
        dc1 = (back(wg, k2_ref, t, inner) * ds2[t]).astype(BF16).astype(F32)
        store_wide(wd, t, dc1)
        kept = jnp.where(mine, dc1[1 : 1 + rows], 0.0)
        own[1, t] = kept
        bias[1] = bias[1] + jnp.sum(flat2(kept), axis=0, keepdims=True)
        bias[0] = bias[0] + jnp.sum(flat2(own[0, t]), axis=0, keepdims=True)

    down = own[1].astype(BF16)
    for kt in range(3):
        for kh in range(3):
            first = 2 - kt
            slab = w1[: frames - first, kh + 1 : kh + 1 + rows]
            term = dot(flat2(slab), flat2(down[first:]), ((0,), (0,)))
            terms[1, (kt * 3 + kh) * 3 * chans : (kt * 3 + kh + 1) * 3 * chans] = term
    tail = terms.shape[1] - taps
    for which in range(2):
        lead = lax.broadcasted_iota(jnp.int32, (tail, chans), 0) == 0
        terms[which, taps:] = jnp.where(lead, bias[which], 0.0)

    for t in range(frames):
        da1 = back(wd, k1_ref, t, rows)[:, :columns]
        z1 = x_ref[t].astype(F32) * s1 + h1
        sig = sigmoid(z1)
        slope = sig * (1.0 + z1 * (1.0 - sig))
        out_ref[t] = (g_ref[t].astype(F32) + da1 * slope * s1).astype(BF16)


def round_up(value, step):
    return -(-value // step) * step


def compute(x, g, k1, b1, k2, s1, h1, s2, h2, recv, sizes, height):
    frames, rows, columns, chans = x.shape
    cols = round_up(columns + 2 * RIM, 16)
    deep = rows + 2 * RIM
    vectors = [v.reshape(1, chans) for v in (b1, s1, h1, s2, h2)]
    return pl.pallas_call(
        functools.partial(compute_kernel, sizes),
        name="compute",
        out_shape=[
            jax.ShapeDtypeStruct(x.shape, BF16),
            jax.ShapeDtypeStruct((2, height, chans), F32),
        ],
        in_specs=[VMEM] * 17,
        out_specs=[VMEM] * 2,
        scratch_shapes=[
            pltpu.VMEM((2, frames, deep, cols, chans), F32),
            pltpu.VMEM((frames, deep, cols, 3 * chans), BF16),
            pltpu.VMEM((frames, deep, cols, 3 * chans), BF16),
            pltpu.VMEM((frames, rows + 2, cols, 3 * chans), BF16),
            pltpu.VMEM((frames, rows + 2, cols, 3 * chans), BF16),
            pltpu.VMEM((frames, rows + 2, cols, chans), F32),
            pltpu.VMEM((2, frames, rows, cols, chans), F32),
        ],
    )(x, g, k1, vectors[0], k2, *vectors[1:], *recv)


def reduce_kernel(sizes, factor, taps, in_ref, *refs):
    outs = refs[:4]
    half_send, half_recv, part_send, part_recv, piece_send, piece_recv, summed, full = refs[4:12]
    sems = refs[12:]
    ha, wa = lax.axis_index("ha"), lax.axis_index("wa")
    core, mid, outer = lax.rem(wa, 2), lax.rem(wa // 2, 2), wa // 4
    many_b, many_c = 2 * sizes[0], sizes[1] // 4
    b = ha * 2 + mid
    height = in_ref.shape[1]
    half = height // 2
    part = half // many_b
    piece = part // many_c

    def in_b(j):
        q = lax.rem(b + j, many_b)
        return q, (q // 2, outer * 4 + lax.rem(q, 2) * 2 + core)

    def in_c(j):
        q = lax.rem(outer + j, many_c)
        return q, (ha, q * 4 + mid * 2 + core)

    partner = (ha, wa + 1 - 2 * core)
    barrier = pltpu.get_barrier_semaphore()
    peers = [partner] + [in_b(j)[1] for j in range(1, many_b)]
    peers += [in_c(j)[1] for j in range(1, many_c)]
    for there in peers:
        pl.semaphore_signal(barrier, inc=1, device_id=there, device_id_type=MESH)

    def rows_at(start, size):
        return pl.ds(pl.multiple_of(start, 16), size)

    def send(src, dst, stage, which, slot, there):
        copy = pltpu.make_async_remote_copy(
            src_ref=src,
            dst_ref=dst,
            send_sem=sems[2 * stage].at[which, slot],
            recv_sem=sems[2 * stage + 1].at[which, slot],
            device_id=there,
            device_id_type=MESH,
        )
        copy.start()
        return copy

    copies = {}
    for w in range(2):
        half_send[w] = in_ref[w, rows_at((1 - core) * half, half)].astype(BF16)
        if w == 0:
            pl.semaphore_wait(barrier, len(peers))
        copies["a", w] = [send(half_send.at[w], half_recv.at[w], 0, w, 0, partner)]
    for w in range(2):
        copies["a", w][0].wait_recv()
        total = in_ref[w, rows_at(core * half, half)] + half_recv[w].astype(F32)
        summed[w] = total
        part_send[w] = total.astype(BF16)
        copies["b", w] = []
        for j in range(1, many_b):
            q, there = in_b(j)
            copies["b", w].append(
                send(
                    part_send.at[w, rows_at(q * part, part)],
                    part_recv.at[w, j - 1],
                    1,
                    w,
                    j - 1,
                    there,
                )
            )
    for w in range(2):
        total = summed[w, rows_at(b * part, part)]
        for j in range(1, many_b):
            copies["b", w][j - 1].wait_recv()
            total = total + part_recv[w, j - 1].astype(F32)
        summed[w, :part] = total
        piece_send[w] = total.astype(BF16)
        copies["c", w] = []
        for j in range(1, many_c):
            q, there = in_c(j)
            copies["c", w].append(
                send(
                    piece_send.at[w, rows_at(q * piece, piece)],
                    piece_recv.at[w, j - 1],
                    2,
                    w,
                    j - 1,
                    there,
                )
            )
    part_at = core * half + b * part
    for w in range(2):
        total = summed[w, rows_at(outer * piece, piece)]
        for j in range(1, many_c):
            copies["c", w][j - 1].wait_recv()
            total = total + piece_recv[w, j - 1].astype(F32)
        here = rows_at(part_at + outer * piece, piece)
        full[w, here] = (total * factor).astype(BF16)
        copies["d", w] = [
            send(full.at[w, here], full.at[w, here], 3, w, j - 1, in_c(j)[1])
            for j in range(1, many_c)
        ]
    for w in range(2):
        for copy in copies["d", w]:
            copy.wait_recv()
        here = rows_at(part_at, part)
        copies["e", w] = [
            send(full.at[w, here], full.at[w, here], 4, w, j - 1, in_b(j)[1])
            for j in range(1, many_b)
        ]
    for w in range(2):
        for copy in copies["e", w]:
            copy.wait_recv()
        here = rows_at(core * half, half)
        copies["f", w] = [send(full.at[w, here], full.at[w, here], 5, w, 0, partner)]
    for w in range(2):
        copies["f", w][0].wait_recv()
        outs[w][...] = full[w, :taps].astype(F32)
        outs[2 + w][...] = full[w, taps : taps + 16].astype(F32)[:1]
    for group in copies.values():
        for copy in group:
            copy.wait_send()


def all_reduce(terms, sizes, factor, taps):
    _, height, chans = terms.shape
    many_b, many_c = 2 * sizes[0], sizes[1] // 4
    half = height // 2
    part = half // many_b
    piece = part // many_c
    slots = [1, many_b - 1, many_c - 1, many_c - 1, many_b - 1, 1]
    return pl.pallas_call(
        functools.partial(reduce_kernel, sizes, factor, taps),
        name="reduce",
        out_shape=[jax.ShapeDtypeStruct((taps, chans), F32)] * 2
        + [jax.ShapeDtypeStruct((1, chans), F32)] * 2,
        in_specs=[VMEM],
        out_specs=[VMEM] * 4,
        scratch_shapes=[
            pltpu.VMEM((2, half, chans), BF16),
            pltpu.VMEM((2, half, chans), BF16),
            pltpu.VMEM((2, half, chans), BF16),
            pltpu.VMEM((2, many_b - 1, part, chans), BF16),
            pltpu.VMEM((2, part, chans), BF16),
            pltpu.VMEM((2, many_c - 1, piece, chans), BF16),
            pltpu.VMEM((2, half, chans), F32),
            pltpu.VMEM((2, height, chans), BF16),
        ]
        + [pltpu.SemaphoreType.DMA((2, n)) for n in slots for _ in range(2)],
        compiler_params=pltpu.CompilerParams(collective_id=1, has_side_effects=True),
    )(terms)


def body(sizes, x, g, k1, b1, k2, s1, h1, s2, h2):
    frames, rows, columns, chans = x.shape
    factor = 1.0 / math.sqrt(frames * rows * sizes[0] * columns * sizes[1])
    taps = 27 * chans
    height = round_up(taps + 16, 16 * sizes[0] * sizes[1])
    recv = halo(x, g, sizes)
    grad_input, terms = compute(x, g, k1, b1, k2, s1, h1, s2, h2, recv, sizes, height)
    grad_two, grad_one, bias_b, bias_a = all_reduce(terms, sizes, factor, taps)
    return (
        grad_input,
        grad_one.reshape(k1.shape),
        bias_a.reshape(chans),
        grad_two.reshape(k2.shape),
        bias_b.reshape(chans),
    )


def solution(mesh):
    sizes = (mesh.shape["ha"], mesh.shape["wa"])
    cells = P(None, "ha", "wa", None)
    return jax.shard_map(
        functools.partial(body, sizes),
        mesh=mesh,
        in_specs=(cells, cells) + (P(),) * 7,
        out_specs=(cells, P(), P(), P(), P()),
        check_vma=False,
    )
```

```python
import functools
import math

import jax
import jax.numpy as jnp
from jax import lax
from jax.experimental import pallas as pl
from jax.experimental.pallas import tpu as pltpu
from jax.sharding import PartitionSpec as P

MESH = pl.DeviceIdType.MESH
F32 = jnp.float32
BF16 = jnp.bfloat16
VMEM = pl.BlockSpec(memory_space=pltpu.VMEM)
DIRECTIONS = [(dy, dx) for dy in (-1, 0, 1) for dx in (-1, 0, 1) if (dy, dx) != (0, 0)]
RIM = 2


def span(step, size):
    return {-1: (0, RIM), 0: (0, size), 1: (size - RIM, size)}[step]


def rim_shape(direction, frames, rows, columns, chans):
    dy, dx = direction
    return (2 * frames, rows if dy == 0 else RIM, columns if dx == 0 else RIM, chans)


def neighbour(direction, me, sizes):
    there = [m + d for m, d in zip(me, direction)]
    exists = True
    for place, size, d in zip(there, sizes, direction):
        if d < 0:
            exists = jnp.logical_and(exists, place >= 0)
        if d > 0:
            exists = jnp.logical_and(exists, place < size)
    return exists, (there[1], there[0])


def sigmoid(value):
    return 1.0 / (1.0 + jnp.exp(-value))


def store_wide(wide, t, value):
    rows, cols, chans = value.shape
    flat = value.reshape(rows * cols, chans)
    for kw in range(3):
        moved = flat if kw == 0 else pltpu.roll(flat, rows * cols - kw, 0)
        wide[t, :, :, kw * chans : (kw + 1) * chans] = moved.reshape(rows, cols, chans).astype(BF16)


def flat2(value):
    return value.reshape(-1, value.shape[-1])


def dot(a, b, dims):
    return lax.dot_general(a, b, (dims, ((), ())), preferred_element_type=F32)


def round_up(value, step):
    return -(-value // step) * step


def rows_at(start, size):
    return pl.ds(pl.multiple_of(start, 16), size)


class Reducer:
    def __init__(self, sizes, factor, terms, refs, sems, full):
        self.factor, self.terms, self.full, self.sems = factor, terms, full, sems
        (
            self.half_send,
            self.half_recv,
            self.part_send,
            self.part_recv,
            self.piece_send,
            self.piece_recv,
            self.summed,
        ) = refs
        self.ha, self.wa = lax.axis_index("ha"), lax.axis_index("wa")
        self.core = lax.rem(self.wa, 2)
        self.mid = lax.rem(self.wa // 2, 2)
        self.outer = self.wa // 4
        self.many_b, self.many_c = 2 * sizes[0], sizes[1] // 4
        self.b = self.ha * 2 + self.mid
        self.half = terms.shape[1] // 2
        self.part = self.half // self.many_b
        self.piece = self.part // self.many_c
        self.partner = (self.ha, self.wa + 1 - 2 * self.core)
        self.peers = [self.partner]
        self.peers += [self.in_b(j)[1] for j in range(1, self.many_b)]
        self.peers += [self.in_c(j)[1] for j in range(1, self.many_c)]
        self.copies = {}

    def in_b(self, j):
        q = lax.rem(self.b + j, self.many_b)
        return q, (q // 2, self.outer * 4 + lax.rem(q, 2) * 2 + self.core)

    def in_c(self, j):
        q = lax.rem(self.outer + j, self.many_c)
        return q, (self.ha, q * 4 + self.mid * 2 + self.core)

    def send(self, src, dst, stage, which, slot, there):
        copy = pltpu.make_async_remote_copy(
            src_ref=src,
            dst_ref=dst,
            send_sem=self.sems[2 * stage].at[which, slot],
            recv_sem=self.sems[2 * stage + 1].at[which, slot],
            device_id=there,
            device_id_type=MESH,
        )
        copy.start()
        self.copies.setdefault((stage, which), []).append(copy)

    def arrive(self, stage, which):
        for copy in self.copies[stage, which]:
            copy.wait_recv()

    def start(self, w):
        half = self.half
        self.half_send[w] = self.terms[w, rows_at((1 - self.core) * half, half)].astype(BF16)
        self.send(self.half_send.at[w], self.half_recv.at[w], 0, w, 0, self.partner)

    def halves(self, w):
        self.arrive(0, w)
        total = self.terms[w, rows_at(self.core * self.half, self.half)]
        total = total + self.half_recv[w].astype(F32)
        self.summed[w] = total
        self.part_send[w] = total.astype(BF16)
        for j in range(1, self.many_b):
            q, there = self.in_b(j)
            src = self.part_send.at[w, rows_at(q * self.part, self.part)]
            self.send(src, self.part_recv.at[w, j - 1], 1, w, j - 1, there)

    def parts(self, w):
        total = self.summed[w, rows_at(self.b * self.part, self.part)]
        self.arrive(1, w)
        for j in range(1, self.many_b):
            total = total + self.part_recv[w, j - 1].astype(F32)
        self.summed[w, : self.part] = total
        self.piece_send[w] = total.astype(BF16)
        for j in range(1, self.many_c):
            q, there = self.in_c(j)
            src = self.piece_send.at[w, rows_at(q * self.piece, self.piece)]
            self.send(src, self.piece_recv.at[w, j - 1], 2, w, j - 1, there)

    def pieces(self, w):
        total = self.summed[w, rows_at(self.outer * self.piece, self.piece)]
        self.arrive(2, w)
        for j in range(1, self.many_c):
            total = total + self.piece_recv[w, j - 1].astype(F32)
        start = self.core * self.half + self.b * self.part + self.outer * self.piece
        here = rows_at(start, self.piece)
        self.full[w, here] = (total * self.factor).astype(BF16)
        for j in range(1, self.many_c):
            self.spread(w, here, 3, j, self.in_c(j)[1])

    def spread(self, w, here, stage, j, there):
        self.send(self.full.at[w, here], self.full.at[w, here], stage, w, j - 1, there)

    def join_pieces(self, w):
        self.arrive(3, w)
        here = rows_at(self.core * self.half + self.b * self.part, self.part)
        for j in range(1, self.many_b):
            self.spread(w, here, 4, j, self.in_b(j)[1])

    def join_parts(self, w):
        self.arrive(4, w)
        here = rows_at(self.core * self.half, self.half)
        self.spread(w, here, 5, 1, self.partner)

    def finish(self, w):
        self.arrive(5, w)
        for stage in range(6):
            for copy in self.copies[stage, w]:
                copy.wait_send()


def block_kernel(
    sizes,
    factor,
    x_ref,
    g_ref,
    k1_hbm,
    b1_ref,
    k2_hbm,
    s1_ref,
    h1_ref,
    s2_ref,
    h2_ref,
    out_ref,
    full,
    *refs,
):
    recv, stage = refs[:8], refs[8:16]
    send_sem, recv_sem, load_sem, k1_ref, k2_ref = refs[16:21]
    pad, w1, wg, w2, wd, ds2, own, terms = refs[21:29]
    reducer = Reducer(sizes, factor, terms, refs[29:36], refs[36:], full)
    frames, rows, columns, chans = x_ref.shape
    deep, cols = pad.shape[2:4]
    inner = rows + 2
    taps = 27 * chans
    grid = (sizes[1], sizes[0])
    me = (lax.axis_index("wa"), lax.axis_index("ha"))
    loads = [
        pltpu.make_async_copy(k1_hbm, k1_ref, load_sem.at[0]),
        pltpu.make_async_copy(k2_hbm, k2_ref, load_sem.at[1]),
    ]
    for load in loads:
        load.start()

    barrier = pltpu.get_barrier_semaphore()
    places = [neighbour(d, me, grid) for d in DIRECTIONS]
    for exists, there in places:

        @pl.when(exists)
        def _(there=there):
            pl.semaphore_signal(barrier, inc=1, device_id=there, device_id_type=MESH)

    for there in reducer.peers:
        pl.semaphore_signal(barrier, inc=1, device_id=there, device_id_type=MESH)
    for which, ref in enumerate((x_ref, g_ref)):
        whole = ref[...].astype(F32)
        for k, (dr, dc) in enumerate(DIRECTIONS):
            r0, r1 = span(dr, rows)
            c0, c1 = span(dc, columns)
            stage[k][which * frames : (which + 1) * frames] = whole[:, r0:r1, c0:c1].astype(BF16)
    count = sum(jnp.where(exists, 1, 0) for exists, _ in places)
    pl.semaphore_wait(barrier, count + len(reducer.peers))
    copies = []
    for k, (exists, there) in enumerate(places):
        copy = pltpu.make_async_remote_copy(
            src_ref=stage[k],
            dst_ref=recv[7 - k],
            send_sem=send_sem.at[k],
            recv_sem=recv_sem.at[7 - k],
            device_id=there,
            device_id_type=MESH,
        )
        pl.when(exists)(copy.start)
        copies.append(copy)

    pad[...] = jnp.zeros_like(pad)
    pad[0, :, RIM : RIM + rows, RIM : RIM + columns] = x_ref[...].astype(F32)
    pad[1, :, RIM : RIM + rows, RIM : RIM + columns] = g_ref[...].astype(F32)
    for t in range(frames):
        own[0, t] = jnp.zeros_like(own[0, t])
        own[0, t, :, :columns] = g_ref[t].astype(F32)

    starts = {-1: 0, 0: RIM}
    for k, direction in enumerate(DIRECTIONS):
        exists, there = places[k]
        r0 = starts.get(direction[0], RIM + rows)
        c0 = starts.get(direction[1], RIM + columns)
        _, nr, nc, _ = recv[k].shape

        @pl.when(exists)
        def _(k=k, there=there, r0=r0, c0=c0, nr=nr, nc=nc):
            copies[k].wait_send()
            pltpu.make_async_remote_copy(
                src_ref=stage[k],
                dst_ref=recv[k],
                send_sem=send_sem.at[k],
                recv_sem=recv_sem.at[k],
                device_id=there,
                device_id_type=MESH,
            ).wait_recv()
            value = recv[k][...].astype(F32)
            for which in range(2):
                pad[which, :, r0 : r0 + nr, c0 : c0 + nc] = value[
                    which * frames : (which + 1) * frames
                ]

    def inside(depth, wide, rim):
        shape = (depth, cols, chans)
        r = lax.broadcasted_iota(jnp.int32, shape, 0) + (me[0] * rows - rim)
        c = lax.broadcasted_iota(jnp.int32, shape, 1)
        place = c + (me[1] * columns - rim)
        ok = (r >= 0) & (r < rows * grid[0]) & (place >= 0) & (place < columns * grid[1])
        return ok & (c < wide)

    s1, h1, s2, h2 = s1_ref[...], h1_ref[...], s2_ref[...], h2_ref[...]
    ok1 = inside(deep, columns + 2 * RIM, RIM)
    for t in range(frames):
        z1 = pad[0, t] * s1 + h1
        store_wide(w1, t, jnp.where(ok1, z1 * sigmoid(z1), 0.0))
        store_wide(wg, t, pad[1, t])

    loads[0].wait()
    ok2 = inside(inner, columns + 2, 1)
    for t in range(frames):
        total = jnp.zeros((inner * cols, chans), F32)
        for kt in range(max(2 - t, 0), 3):
            for kw in range(3):
                weights = jnp.concatenate([k1_ref[kt, kh, kw] for kh in range(3)], axis=0)
                total = total + dot(
                    flat2(w1[t + kt - 2, kw : kw + inner]), weights, ((1,), (0,))
                )
        z2 = (total.reshape(inner, cols, chans) + b1_ref[...]) * s2 + h2
        sig = sigmoid(z2)
        store_wide(w2, t, jnp.where(ok2, z2 * sig, 0.0))
        ds2[t] = jnp.where(ok2, sig * (1.0 + z2 * (1.0 - sig)) * s2, 0.0)

    def kernel_terms(which, wide, skip, grads):
        for kt in range(3):
            first = 2 - kt
            for kw in range(3):
                slab = wide[: frames - first, kw + skip : kw + skip + rows]
                term = dot(flat2(slab), flat2(grads[first:]), ((0,), (0,)))
                for kh in range(3):
                    at = (kt * 9 + kh * 3 + kw) * chans
                    terms[which, at : at + chans] = term[kh * chans : (kh + 1) * chans]
        bias = jnp.sum(flat2(own[which]), axis=0, keepdims=True)
        tail = terms.shape[1] - taps
        lead = lax.broadcasted_iota(jnp.int32, (tail, chans), 0) == 0
        terms[which, taps:] = jnp.where(lead, bias, 0.0)

    kernel_terms(0, w2, 0, own[0].astype(BF16))
    reducer.start(0)

    def back(wide, kernel_ref, t, depth):
        total = jnp.zeros((depth * cols, chans), F32)
        for kt in range(t, 3):
            for kw in range(3):
                weights = jnp.concatenate(
                    [kernel_ref[kt, 2 - kh, 2 - kw] for kh in range(3)], axis=1
                )
                total = total + dot(
                    flat2(wide[t + 2 - kt, kw : kw + depth]), weights, ((1,), (1,))
                )
        return total.reshape(depth, cols, chans)

    loads[1].wait()
    c = lax.broadcasted_iota(jnp.int32, (rows, cols, chans), 1)
    mine = (c >= 1) & (c <= columns)
    for t in range(frames):
        dc1 = (back(wg, k2_ref, t, inner) * ds2[t]).astype(BF16).astype(F32)
        store_wide(wd, t, dc1)
        own[1, t] = jnp.where(mine, dc1[1 : 1 + rows], 0.0)

    reducer.halves(0)
    kernel_terms(1, w1, 1, own[1].astype(BF16))
    reducer.start(1)

    def input_grad(t):
        da1 = back(wd, k1_ref, t, rows)[:, :columns]
        z1 = x_ref[t].astype(F32) * s1 + h1
        sig = sigmoid(z1)
        slope = sig * (1.0 + z1 * (1.0 - sig))
        out_ref[t] = (g_ref[t].astype(F32) + da1 * slope * s1).astype(BF16)

    input_grad(0)
    reducer.halves(1)
    reducer.parts(0)
    for t in range(1, frames):
        input_grad(t)
    reducer.pieces(0)
    reducer.parts(1)
    reducer.join_pieces(0)
    reducer.pieces(1)
    reducer.join_parts(0)
    reducer.join_pieces(1)
    reducer.join_parts(1)
    for w in range(2):
        reducer.finish(w)


def widen_kernel(taps, full, x_ref, two_ref, one_ref, bias_two_ref, bias_one_ref, y_ref):
    for w, (out_ref, bias_ref) in enumerate(((two_ref, bias_two_ref), (one_ref, bias_one_ref))):
        out_ref[...] = full[w, :taps].astype(F32)
        bias_ref[...] = full[w, taps : taps + 16].astype(F32)[0]
    y_ref[...] = x_ref[...]


def body(sizes, x, g, k1, b1, k2, s1, h1, s2, h2):
    x, g = (jnp.transpose(v, (0, 2, 1, 3)) for v in (x, g))
    frames, rows, columns, chans = x.shape
    factor = 1.0 / math.sqrt(frames * rows * sizes[1] * columns * sizes[0])
    taps = 27 * chans
    height = round_up(taps + 16, 16 * sizes[0] * sizes[1])
    cols = round_up(columns + 2 * RIM, 16)
    deep, inner = rows + 2 * RIM, rows + 2
    many_b, many_c = 2 * sizes[0], sizes[1] // 4
    half = height // 2
    part = half // many_b
    piece = part // many_c
    slots = [1, many_b - 1, many_c - 1, many_c - 1, many_b - 1, 1]
    rims = [pltpu.VMEM(rim_shape(d, frames, rows, columns, chans), BF16) for d in DIRECTIONS]
    vectors = [v.reshape(1, chans) for v in (b1, s1, h1, s2, h2)]
    hbm = pl.BlockSpec(memory_space=pl.ANY)
    grad_input, full = pl.pallas_call(
        functools.partial(block_kernel, sizes, factor),
        name="block",
        out_shape=[
            jax.ShapeDtypeStruct(x.shape, BF16),
            jax.ShapeDtypeStruct((2, height, chans), BF16),
        ],
        in_specs=[VMEM, VMEM, hbm, VMEM, hbm] + [VMEM] * 4,
        out_specs=[VMEM] * 2,
        scratch_shapes=rims
        + rims
        + [pltpu.SemaphoreType.DMA((8,)), pltpu.SemaphoreType.DMA((8,))]
        + [pltpu.SemaphoreType.DMA((2,)), pltpu.VMEM(k1.shape, BF16), pltpu.VMEM(k2.shape, BF16)]
        + [
            pltpu.VMEM((2, frames, deep, cols, chans), F32),
            pltpu.VMEM((frames, deep, cols, 3 * chans), BF16),
            pltpu.VMEM((frames, deep, cols, 3 * chans), BF16),
            pltpu.VMEM((frames, inner, cols, 3 * chans), BF16),
            pltpu.VMEM((frames, inner, cols, 3 * chans), BF16),
            pltpu.VMEM((frames, inner, cols, chans), F32),
            pltpu.VMEM((2, frames, rows, cols, chans), F32),
            pltpu.VMEM((2, height, chans), F32),
        ]
        + [
            pltpu.VMEM((2, half, chans), BF16),
            pltpu.VMEM((2, half, chans), BF16),
            pltpu.VMEM((2, half, chans), BF16),
            pltpu.VMEM((2, many_b - 1, part, chans), BF16),
            pltpu.VMEM((2, part, chans), BF16),
            pltpu.VMEM((2, many_c - 1, piece, chans), BF16),
            pltpu.VMEM((2, half, chans), F32),
        ]
        + [pltpu.SemaphoreType.DMA((2, n)) for n in slots for _ in range(2)],
        compiler_params=pltpu.CompilerParams(collective_id=0, has_side_effects=True),
    )(x, g, k1, vectors[0], k2, *vectors[1:])
    grad_two, grad_one, bias_two, bias_one, grad_input = pl.pallas_call(
        functools.partial(widen_kernel, taps),
        name="widen",
        out_shape=[jax.ShapeDtypeStruct((taps, chans), F32)] * 2
        + [jax.ShapeDtypeStruct((chans,), F32)] * 2
        + [jax.ShapeDtypeStruct(x.shape, BF16)],
        in_specs=[VMEM] * 2,
        out_specs=[VMEM] * 5,
    )(full, grad_input)
    return (
        jnp.transpose(grad_input, (0, 2, 1, 3)),
        grad_one.reshape(k1.shape),
        bias_one,
        grad_two.reshape(k2.shape),
        bias_two,
    )


def solution(mesh):
    sizes = (mesh.shape["ha"], mesh.shape["wa"])
    cells = P(None, "ha", "wa", None)
    return jax.shard_map(
        functools.partial(body, sizes),
        mesh=mesh,
        in_specs=(cells, cells) + (P(),) * 7,
        out_specs=(cells, P(), P(), P(), P()),
        check_vma=False,
    )
```

```python
import functools
import math

import jax
import jax.numpy as jnp
from jax import lax
from jax.experimental import pallas as pl
from jax.experimental.pallas import tpu as pltpu
from jax.sharding import PartitionSpec as P

MESH = pl.DeviceIdType.MESH
F32 = jnp.float32
BF16 = jnp.bfloat16
VMEM = pl.BlockSpec(memory_space=pltpu.VMEM)
DIRECTIONS = [(dy, dx) for dy in (-1, 0, 1) for dx in (-1, 0, 1) if (dy, dx) != (0, 0)]
RIM = 2
GROUPS = 2


def span(step, size):
    return {-1: (0, RIM), 0: (0, size), 1: (size - RIM, size)}[step]


def rim_shape(direction, frames, rows, columns, chans):
    dy, dx = direction
    return (2 * frames, rows if dy == 0 else RIM, columns if dx == 0 else RIM, chans)


def neighbour(direction, me, sizes):
    there = [m + d for m, d in zip(me, direction)]
    exists = True
    for place, size, d in zip(there, sizes, direction):
        if d < 0:
            exists = jnp.logical_and(exists, place >= 0)
        if d > 0:
            exists = jnp.logical_and(exists, place < size)
    return exists, (there[1], there[0])


def sigmoid(value):
    return 1.0 / (1.0 + jnp.exp(-value))


def store_wide(wide, t, value):
    rows, cols, chans = value.shape
    flat = value.reshape(rows * cols, chans)
    for kw in range(3):
        moved = flat if kw == 0 else pltpu.roll(flat, rows * cols - kw, 0)
        wide[t, :, :, kw * chans : (kw + 1) * chans] = moved.reshape(rows, cols, chans).astype(BF16)


def flat2(value):
    return value.reshape(-1, value.shape[-1])


def dot(a, b, dims):
    return lax.dot_general(a, b, (dims, ((), ())), preferred_element_type=F32)


def round_up(value, step):
    return -(-value // step) * step


def rows_at(start, size):
    return pl.ds(pl.multiple_of(start, 8), size)


class Reducer:
    def __init__(self, sizes, factor, terms, refs, sems, full):
        self.factor, self.terms, self.full, self.sems = factor, terms, full, sems
        (
            self.half_send,
            self.half_recv,
            self.part_send,
            self.part_recv,
            self.piece_send,
            self.piece_recv,
            self.summed,
        ) = refs
        self.ha, self.wa = lax.axis_index("ha"), lax.axis_index("wa")
        self.core = lax.rem(self.wa, 2)
        self.mid = lax.rem(self.wa // 2, 2)
        self.outer = self.wa // 4
        self.many_b, self.many_c = 2 * sizes[0], sizes[1] // 4
        self.b = self.ha * 2 + self.mid
        self.half = terms.shape[1] // 2
        self.part = self.half // self.many_b
        self.piece = self.part // self.many_c
        self.partner = (self.ha, self.wa + 1 - 2 * self.core)
        self.peers = [self.partner]
        self.peers += [self.in_b(j)[1] for j in range(1, self.many_b)]
        self.peers += [self.in_c(j)[1] for j in range(1, self.many_c)]
        self.copies = {}

    def in_b(self, j):
        q = lax.rem(self.b + j, self.many_b)
        return q, (q // 2, self.outer * 4 + lax.rem(q, 2) * 2 + self.core)

    def in_c(self, j):
        q = lax.rem(self.outer + j, self.many_c)
        return q, (self.ha, q * 4 + self.mid * 2 + self.core)

    def send(self, src, dst, stage, which, slot, there):
        copy = pltpu.make_async_remote_copy(
            src_ref=src,
            dst_ref=dst,
            send_sem=self.sems[2 * stage].at[which, slot],
            recv_sem=self.sems[2 * stage + 1].at[which, slot],
            device_id=there,
            device_id_type=MESH,
        )
        copy.start()
        self.copies.setdefault((stage, which), []).append(copy)

    def arrive(self, stage, which):
        for copy in self.copies[stage, which]:
            copy.wait_recv()

    def start(self, w):
        half = self.half
        self.half_send[w] = self.terms[w, rows_at((1 - self.core) * half, half)].astype(BF16)
        self.send(self.half_send.at[w], self.half_recv.at[w], 0, w, 0, self.partner)

    def halves(self, w):
        self.arrive(0, w)
        total = self.terms[w, rows_at(self.core * self.half, self.half)]
        total = total + self.half_recv[w].astype(F32)
        self.summed[w] = total
        self.part_send[w] = total.astype(BF16)
        for j in range(1, self.many_b):
            q, there = self.in_b(j)
            src = self.part_send.at[w, rows_at(q * self.part, self.part)]
            self.send(src, self.part_recv.at[w, j - 1], 1, w, j - 1, there)

    def parts(self, w):
        total = self.summed[w, rows_at(self.b * self.part, self.part)]
        self.arrive(1, w)
        for j in range(1, self.many_b):
            total = total + self.part_recv[w, j - 1].astype(F32)
        self.summed[w, : self.part] = total
        self.piece_send[w] = total.astype(BF16)
        for j in range(1, self.many_c):
            q, there = self.in_c(j)
            src = self.piece_send.at[w, rows_at(q * self.piece, self.piece)]
            self.send(src, self.piece_recv.at[w, j - 1], 2, w, j - 1, there)

    def pieces(self, w):
        total = self.summed[w, rows_at(self.outer * self.piece, self.piece)]
        self.arrive(2, w)
        for j in range(1, self.many_c):
            total = total + self.piece_recv[w, j - 1].astype(F32)
        start = self.core * self.half + self.b * self.part + self.outer * self.piece
        here = rows_at(start, self.piece)
        self.full[w, here] = (total * self.factor).astype(BF16)
        for j in range(1, self.many_c):
            self.spread(w, here, 3, j, self.in_c(j)[1])

    def spread(self, w, here, stage, j, there):
        self.send(self.full.at[w, here], self.full.at[w, here], stage, w, j - 1, there)

    def join_pieces(self, w):
        self.arrive(3, w)
        here = rows_at(self.core * self.half + self.b * self.part, self.part)
        for j in range(1, self.many_b):
            self.spread(w, here, 4, j, self.in_b(j)[1])

    def join_parts(self, w):
        self.arrive(4, w)
        here = rows_at(self.core * self.half, self.half)
        self.spread(w, here, 5, 1, self.partner)

    def finish(self, w):
        self.arrive(5, w)
        for stage in range(6):
            for copy in self.copies[stage, w]:
                copy.wait_send()


def block_kernel(
    sizes,
    factor,
    x_ref,
    g_ref,
    k1_hbm,
    b1_ref,
    k2_hbm,
    s1_ref,
    h1_ref,
    s2_ref,
    h2_ref,
    out_ref,
    full,
    *refs,
):
    recv, stage = refs[:8], refs[8:16]
    send_sem, recv_sem, load_sem, k1_ref, k2_ref = refs[16:21]
    pad, w1, wg, w2, wd, ds2, own, terms = refs[21:29]
    reducer = Reducer(sizes, factor, terms, refs[29:36], refs[36:], full)
    frames, rows, columns, chans = x_ref.shape
    deep, cols = pad.shape[2:4]
    inner = rows + 2
    taps = 27 * chans
    grid = (sizes[1], sizes[0])
    me = (lax.axis_index("wa"), lax.axis_index("ha"))
    loads = [
        pltpu.make_async_copy(k1_hbm, k1_ref, load_sem.at[0]),
        pltpu.make_async_copy(k2_hbm, k2_ref, load_sem.at[1]),
    ]
    for load in loads:
        load.start()

    barrier = pltpu.get_barrier_semaphore()
    places = [neighbour(d, me, grid) for d in DIRECTIONS]
    for exists, there in places:

        @pl.when(exists)
        def _(there=there):
            pl.semaphore_signal(barrier, inc=1, device_id=there, device_id_type=MESH)

    for there in reducer.peers:
        pl.semaphore_signal(barrier, inc=1, device_id=there, device_id_type=MESH)
    for which, ref in enumerate((x_ref, g_ref)):
        whole = ref[...].astype(F32)
        for k, (dr, dc) in enumerate(DIRECTIONS):
            r0, r1 = span(dr, rows)
            c0, c1 = span(dc, columns)
            stage[k][which * frames : (which + 1) * frames] = whole[:, r0:r1, c0:c1].astype(BF16)
    count = sum(jnp.where(exists, 1, 0) for exists, _ in places)
    pl.semaphore_wait(barrier, count + len(reducer.peers))
    copies = []
    for k, (exists, there) in enumerate(places):
        copy = pltpu.make_async_remote_copy(
            src_ref=stage[k],
            dst_ref=recv[7 - k],
            send_sem=send_sem.at[k],
            recv_sem=recv_sem.at[7 - k],
            device_id=there,
            device_id_type=MESH,
        )
        pl.when(exists)(copy.start)
        copies.append(copy)

    pad[...] = jnp.zeros_like(pad)
    pad[0, :, RIM : RIM + rows, RIM : RIM + columns] = x_ref[...].astype(F32)
    pad[1, :, RIM : RIM + rows, RIM : RIM + columns] = g_ref[...].astype(F32)
    for t in range(frames):
        own[0, t] = jnp.zeros_like(own[0, t])
        own[0, t, :, :columns] = g_ref[t].astype(F32)

    starts = {-1: 0, 0: RIM}
    for k, direction in enumerate(DIRECTIONS):
        exists, there = places[k]
        r0 = starts.get(direction[0], RIM + rows)
        c0 = starts.get(direction[1], RIM + columns)
        _, nr, nc, _ = recv[k].shape

        @pl.when(exists)
        def _(k=k, there=there, r0=r0, c0=c0, nr=nr, nc=nc):
            copies[k].wait_send()
            pltpu.make_async_remote_copy(
                src_ref=stage[k],
                dst_ref=recv[k],
                send_sem=send_sem.at[k],
                recv_sem=recv_sem.at[k],
                device_id=there,
                device_id_type=MESH,
            ).wait_recv()
            value = recv[k][...].astype(F32)
            for which in range(2):
                pad[which, :, r0 : r0 + nr, c0 : c0 + nc] = value[
                    which * frames : (which + 1) * frames
                ]

    def inside(depth, wide, rim):
        shape = (depth, cols, chans)
        r = lax.broadcasted_iota(jnp.int32, shape, 0) + (me[0] * rows - rim)
        c = lax.broadcasted_iota(jnp.int32, shape, 1)
        place = c + (me[1] * columns - rim)
        ok = (r >= 0) & (r < rows * grid[0]) & (place >= 0) & (place < columns * grid[1])
        return ok & (c < wide)

    s1, h1, s2, h2 = s1_ref[...], h1_ref[...], s2_ref[...], h2_ref[...]
    ok1 = inside(deep, columns + 2 * RIM, RIM)
    for t in range(frames):
        z1 = pad[0, t] * s1 + h1
        store_wide(w1, t, jnp.where(ok1, z1 * sigmoid(z1), 0.0))
        store_wide(wg, t, pad[1, t])

    loads[0].wait()
    ok2 = inside(inner, columns + 2, 1)
    for t in range(frames):
        total = jnp.zeros((inner * cols, chans), F32)
        for kt in range(max(2 - t, 0), 3):
            for kw in range(3):
                weights = jnp.concatenate([k1_ref[kt, kh, kw] for kh in range(3)], axis=0)
                total = total + dot(
                    flat2(w1[t + kt - 2, kw : kw + inner]), weights, ((1,), (0,))
                )
        z2 = (total.reshape(inner, cols, chans) + b1_ref[...]) * s2 + h2
        sig = sigmoid(z2)
        store_wide(w2, t, jnp.where(ok2, z2 * sig, 0.0))
        ds2[t] = jnp.where(ok2, sig * (1.0 + z2 * (1.0 - sig)) * s2, 0.0)

    def put(which, at, value):
        size = terms.shape[1]
        end = at + value.shape[0]
        for k in range(GROUPS):
            low, high = max(at, k * size), min(end, (k + 1) * size)
            if low < high:
                terms[which * GROUPS + k, low - k * size : high - k * size] = value[
                    low - at : high - at
                ]

    def kernel_terms(which, wide, skip, grads):
        for kt in range(3):
            first = 2 - kt
            for kw in range(3):
                slab = wide[: frames - first, kw + skip : kw + skip + rows]
                term = dot(flat2(slab), flat2(grads[first:]), ((0,), (0,)))
                for kh in range(3):
                    at = (kt * 9 + kh * 3 + kw) * chans
                    put(which, at, term[kh * chans : (kh + 1) * chans])
        bias = jnp.sum(flat2(own[which]), axis=0, keepdims=True)
        tail = GROUPS * terms.shape[1] - taps
        lead = lax.broadcasted_iota(jnp.int32, (tail, chans), 0) == 0
        put(which, taps, jnp.where(lead, bias, 0.0))

    kernel_terms(0, w2, 0, own[0].astype(BF16))
    reducer.start(0)
    reducer.start(1)

    def back(wide, kernel_ref, t, depth):
        total = jnp.zeros((depth * cols, chans), F32)
        for kt in range(t, 3):
            for kw in range(3):
                weights = jnp.concatenate(
                    [kernel_ref[kt, 2 - kh, 2 - kw] for kh in range(3)], axis=1
                )
                total = total + dot(
                    flat2(wide[t + 2 - kt, kw : kw + depth]), weights, ((1,), (1,))
                )
        return total.reshape(depth, cols, chans)

    loads[1].wait()
    c = lax.broadcasted_iota(jnp.int32, (rows, cols, chans), 1)
    mine = (c >= 1) & (c <= columns)
    for t in range(frames):
        dc1 = (back(wg, k2_ref, t, inner) * ds2[t]).astype(BF16).astype(F32)
        store_wide(wd, t, dc1)
        own[1, t] = jnp.where(mine, dc1[1 : 1 + rows], 0.0)

    reducer.halves(0)
    reducer.halves(1)
    kernel_terms(1, w1, 1, own[1].astype(BF16))
    reducer.start(2)
    reducer.start(3)

    def input_grad(t):
        da1 = back(wd, k1_ref, t, rows)[:, :columns]
        z1 = x_ref[t].astype(F32) * s1 + h1
        sig = sigmoid(z1)
        slope = sig * (1.0 + z1 * (1.0 - sig))
        out_ref[t] = (g_ref[t].astype(F32) + da1 * slope * s1).astype(BF16)

    input_grad(0)
    reducer.halves(2)
    reducer.halves(3)
    reducer.parts(0)
    input_grad(1)
    reducer.parts(1)
    input_grad(2)
    reducer.pieces(0)
    reducer.pieces(1)
    reducer.parts(2)
    reducer.join_pieces(0)
    reducer.parts(3)
    reducer.join_pieces(1)
    reducer.pieces(2)
    reducer.pieces(3)
    reducer.join_parts(0)
    reducer.join_parts(1)
    reducer.join_pieces(2)
    reducer.join_pieces(3)
    reducer.join_parts(2)
    reducer.join_parts(3)
    for w in range(2 * GROUPS):
        reducer.finish(w)


def widen_kernel(taps, full, x_ref, two_ref, one_ref, bias_two_ref, bias_one_ref, y_ref):
    for w, (out_ref, bias_ref) in enumerate(((two_ref, bias_two_ref), (one_ref, bias_one_ref))):
        out_ref[...] = full[w, :taps].astype(F32)
        bias_ref[...] = full[w, taps : taps + 16].astype(F32)[0]
    y_ref[...] = x_ref[...]


def body(sizes, x, g, k1, b1, k2, s1, h1, s2, h2):
    x, g = (jnp.transpose(v, (0, 2, 1, 3)) for v in (x, g))
    frames, rows, columns, chans = x.shape
    factor = 1.0 / math.sqrt(frames * rows * sizes[1] * columns * sizes[0])
    taps = 27 * chans
    height = round_up(taps + 16, 8 * GROUPS * sizes[0] * sizes[1]) // GROUPS
    cols = round_up(columns + 2 * RIM, 16)
    deep, inner = rows + 2 * RIM, rows + 2
    many_b, many_c = 2 * sizes[0], sizes[1] // 4
    half = height // 2
    part = half // many_b
    piece = part // many_c
    many = 2 * GROUPS
    slots = [1, many_b - 1, many_c - 1, many_c - 1, many_b - 1, 1]
    rims = [pltpu.VMEM(rim_shape(d, frames, rows, columns, chans), BF16) for d in DIRECTIONS]
    vectors = [v.reshape(1, chans) for v in (b1, s1, h1, s2, h2)]
    hbm = pl.BlockSpec(memory_space=pl.ANY)
    grad_input, full = pl.pallas_call(
        functools.partial(block_kernel, sizes, factor),
        name="block",
        out_shape=[
            jax.ShapeDtypeStruct(x.shape, BF16),
            jax.ShapeDtypeStruct((many, height, chans), BF16),
        ],
        in_specs=[VMEM, VMEM, hbm, VMEM, hbm] + [VMEM] * 4,
        out_specs=[VMEM] * 2,
        scratch_shapes=rims
        + rims
        + [pltpu.SemaphoreType.DMA((8,)), pltpu.SemaphoreType.DMA((8,))]
        + [pltpu.SemaphoreType.DMA((2,)), pltpu.VMEM(k1.shape, BF16), pltpu.VMEM(k2.shape, BF16)]
        + [
            pltpu.VMEM((2, frames, deep, cols, chans), F32),
            pltpu.VMEM((frames, deep, cols, 3 * chans), BF16),
            pltpu.VMEM((frames, deep, cols, 3 * chans), BF16),
            pltpu.VMEM((frames, inner, cols, 3 * chans), BF16),
            pltpu.VMEM((frames, inner, cols, 3 * chans), BF16),
            pltpu.VMEM((frames, inner, cols, chans), F32),
            pltpu.VMEM((2, frames, rows, cols, chans), F32),
            pltpu.VMEM((many, height, chans), F32),
        ]
        + [
            pltpu.VMEM((many, half, chans), BF16),
            pltpu.VMEM((many, half, chans), BF16),
            pltpu.VMEM((many, half, chans), BF16),
            pltpu.VMEM((many, many_b - 1, part, chans), BF16),
            pltpu.VMEM((many, part, chans), BF16),
            pltpu.VMEM((many, many_c - 1, piece, chans), BF16),
            pltpu.VMEM((many, half, chans), F32),
        ]
        + [pltpu.SemaphoreType.DMA((many, n)) for n in slots for _ in range(2)],
        compiler_params=pltpu.CompilerParams(collective_id=0, has_side_effects=True),
    )(x, g, k1, vectors[0], k2, *vectors[1:])
    grad_two, grad_one, bias_two, bias_one, grad_input = pl.pallas_call(
        functools.partial(widen_kernel, taps),
        name="widen",
        out_shape=[jax.ShapeDtypeStruct((taps, chans), F32)] * 2
        + [jax.ShapeDtypeStruct((chans,), F32)] * 2
        + [jax.ShapeDtypeStruct(x.shape, BF16)],
        in_specs=[VMEM] * 2,
        out_specs=[VMEM] * 5,
    )(full.reshape(2, GROUPS * height, chans), grad_input)
    return (
        jnp.transpose(grad_input, (0, 2, 1, 3)),
        grad_one.reshape(k1.shape),
        bias_one,
        grad_two.reshape(k2.shape),
        bias_two,
    )


def solution(mesh):
    sizes = (mesh.shape["ha"], mesh.shape["wa"])
    cells = P(None, "ha", "wa", None)
    return jax.shard_map(
        functools.partial(body, sizes),
        mesh=mesh,
        in_specs=(cells, cells) + (P(),) * 7,
        out_specs=(cells, P(), P(), P(), P()),
        check_vma=False,
    )
```

```python
import functools
import math

import jax
import jax.numpy as jnp
from jax import lax
from jax.experimental import pallas as pl
from jax.experimental.pallas import tpu as pltpu
from jax.sharding import PartitionSpec as P

MESH = pl.DeviceIdType.MESH
F32 = jnp.float32
BF16 = jnp.bfloat16
VMEM = pl.BlockSpec(memory_space=pltpu.VMEM)
DIRECTIONS = [(dy, dx) for dy in (-1, 0, 1) for dx in (-1, 0, 1) if (dy, dx) != (0, 0)]
RIM = 2
GROUPS = 2


def span(step, size):
    return {-1: (0, RIM), 0: (0, size), 1: (size - RIM, size)}[step]


def rim_shape(direction, frames, rows, columns, chans):
    dy, dx = direction
    return (2 * frames, rows if dy == 0 else RIM, columns if dx == 0 else RIM, chans)


def neighbour(direction, me, sizes):
    there = [m + d for m, d in zip(me, direction)]
    exists = True
    for place, size, d in zip(there, sizes, direction):
        if d < 0:
            exists = jnp.logical_and(exists, place >= 0)
        if d > 0:
            exists = jnp.logical_and(exists, place < size)
    return exists, (there[1], there[0])


def sigmoid(value):
    return 1.0 / (1.0 + jnp.exp(-value))


def store_wide(wide, t, value):
    rows, cols, chans = value.shape
    flat = value.reshape(rows * cols, chans)
    for kw in range(3):
        moved = flat if kw == 0 else pltpu.roll(flat, rows * cols - kw, 0)
        wide[t, :, :, kw * chans : (kw + 1) * chans] = moved.reshape(rows, cols, chans).astype(BF16)


def flat2(value):
    return value.reshape(-1, value.shape[-1])


def dot(a, b, dims):
    return lax.dot_general(a, b, (dims, ((), ())), preferred_element_type=F32)


def round_up(value, step):
    return -(-value // step) * step


def rows_at(start, size):
    return pl.ds(pl.multiple_of(start, 8), size)


class Reducer:
    def __init__(self, sizes, factor, terms, refs, sems, full):
        self.factor, self.terms, self.full, self.sems = factor, terms, full, sems
        (
            self.half_send,
            self.half_recv,
            self.part_send,
            self.part_recv,
            self.piece_send,
            self.piece_recv,
            self.summed,
        ) = refs
        self.ha, self.wa = lax.axis_index("ha"), lax.axis_index("wa")
        self.core = lax.rem(self.wa, 2)
        self.mid = lax.rem(self.wa // 2, 2)
        self.outer = self.wa // 4
        self.many_b, self.many_c = 2 * sizes[0], sizes[1] // 4
        self.b = self.ha * 2 + self.mid
        self.half = terms.shape[1] // 2
        self.part = self.half // self.many_b
        self.piece = self.part // self.many_c
        self.partner = (self.ha, self.wa + 1 - 2 * self.core)
        self.peers = [self.partner]
        self.peers += [self.in_b(j)[1] for j in range(1, self.many_b)]
        self.peers += [self.in_c(j)[1] for j in range(1, self.many_c)]
        self.copies = {}

    def in_b(self, j):
        q = lax.rem(self.b + j, self.many_b)
        return q, (q // 2, self.outer * 4 + lax.rem(q, 2) * 2 + self.core)

    def in_c(self, j):
        q = lax.rem(self.outer + j, self.many_c)
        return q, (self.ha, q * 4 + self.mid * 2 + self.core)

    def send(self, src, dst, stage, which, slot, there):
        copy = pltpu.make_async_remote_copy(
            src_ref=src,
            dst_ref=dst,
            send_sem=self.sems[2 * stage].at[which, slot],
            recv_sem=self.sems[2 * stage + 1].at[which, slot],
            device_id=there,
            device_id_type=MESH,
        )
        copy.start()
        self.copies.setdefault((stage, which), []).append(copy)

    def arrive(self, stage, which):
        for copy in self.copies[stage, which]:
            copy.wait_recv()

    def start(self, w):
        half = self.half
        self.half_send[w] = self.terms[w, rows_at((1 - self.core) * half, half)].astype(BF16)
        self.send(self.half_send.at[w], self.half_recv.at[w], 0, w, 0, self.partner)

    def halves(self, w):
        self.arrive(0, w)
        total = self.terms[w, rows_at(self.core * self.half, self.half)]
        total = total + self.half_recv[w].astype(F32)
        self.summed[w] = total
        self.part_send[w] = total.astype(BF16)
        for j in range(1, self.many_b):
            q, there = self.in_b(j)
            src = self.part_send.at[w, rows_at(q * self.part, self.part)]
            self.send(src, self.part_recv.at[w, j - 1], 1, w, j - 1, there)

    def parts(self, w):
        total = self.summed[w, rows_at(self.b * self.part, self.part)]
        self.arrive(1, w)
        for j in range(1, self.many_b):
            total = total + self.part_recv[w, j - 1].astype(F32)
        self.summed[w, : self.part] = total
        self.piece_send[w] = total.astype(BF16)
        for j in range(1, self.many_c):
            q, there = self.in_c(j)
            src = self.piece_send.at[w, rows_at(q * self.piece, self.piece)]
            self.send(src, self.piece_recv.at[w, j - 1], 2, w, j - 1, there)

    def pieces(self, w):
        total = self.summed[w, rows_at(self.outer * self.piece, self.piece)]
        self.arrive(2, w)
        for j in range(1, self.many_c):
            total = total + self.piece_recv[w, j - 1].astype(F32)
        start = self.core * self.half + self.b * self.part + self.outer * self.piece
        here = rows_at(start, self.piece)
        self.full[w, here] = (total * self.factor).astype(BF16)
        for j in range(1, self.many_c):
            self.spread(w, here, 3, j, self.in_c(j)[1])

    def spread(self, w, here, stage, j, there):
        self.send(self.full.at[w, here], self.full.at[w, here], stage, w, j - 1, there)

    def part_rows(self, q):
        return rows_at(self.core * self.half + q * self.part, self.part)

    def join_pieces(self, w):
        self.arrive(3, w)
        here = self.part_rows(self.b)
        for j in range(1, self.many_b):
            self.spread(w, here, 4, j, self.in_b(j)[1])
        self.spread(w, here, 5, 1, self.partner)

    def join_parts(self, w):
        for j in range(1, self.many_b):
            self.copies[4, w][j - 1].wait_recv()
            here = self.part_rows(lax.rem(self.b + self.many_b - j, self.many_b))
            self.spread(w, here, 5, j + 1, self.partner)

    def finish(self, w):
        self.arrive(5, w)
        for stage in range(6):
            for copy in self.copies[stage, w]:
                copy.wait_send()


def block_kernel(
    sizes,
    factor,
    x_ref,
    g_ref,
    k1_hbm,
    b1_ref,
    k2_hbm,
    s1_ref,
    h1_ref,
    s2_ref,
    h2_ref,
    out_ref,
    full,
    *refs,
):
    recv, stage = refs[:8], refs[8:16]
    send_sem, recv_sem, load_sem, k1_ref, k2_ref = refs[16:21]
    pad, w1, wg, w2, wd, ds2, own, terms = refs[21:29]
    reducer = Reducer(sizes, factor, terms, refs[29:36], refs[36:], full)
    frames, rows, columns, chans = x_ref.shape
    deep, cols = pad.shape[2:4]
    inner = rows + 2
    taps = 27 * chans
    grid = (sizes[1], sizes[0])
    me = (lax.axis_index("wa"), lax.axis_index("ha"))
    loads = [
        pltpu.make_async_copy(k1_hbm, k1_ref, load_sem.at[0]),
        pltpu.make_async_copy(k2_hbm, k2_ref, load_sem.at[1]),
    ]
    for load in loads:
        load.start()

    barrier = pltpu.get_barrier_semaphore()
    places = [neighbour(d, me, grid) for d in DIRECTIONS]
    for exists, there in places:

        @pl.when(exists)
        def _(there=there):
            pl.semaphore_signal(barrier, inc=1, device_id=there, device_id_type=MESH)

    for there in reducer.peers:
        pl.semaphore_signal(barrier, inc=1, device_id=there, device_id_type=MESH)
    for which, ref in enumerate((x_ref, g_ref)):
        whole = ref[...].astype(F32)
        for k, (dr, dc) in enumerate(DIRECTIONS):
            r0, r1 = span(dr, rows)
            c0, c1 = span(dc, columns)
            stage[k][which * frames : (which + 1) * frames] = whole[:, r0:r1, c0:c1].astype(BF16)
    count = sum(jnp.where(exists, 1, 0) for exists, _ in places)
    pl.semaphore_wait(barrier, count + len(reducer.peers))
    copies = []
    for k, (exists, there) in enumerate(places):
        copy = pltpu.make_async_remote_copy(
            src_ref=stage[k],
            dst_ref=recv[7 - k],
            send_sem=send_sem.at[k],
            recv_sem=recv_sem.at[7 - k],
            device_id=there,
            device_id_type=MESH,
        )
        pl.when(exists)(copy.start)
        copies.append(copy)

    pad[...] = jnp.zeros_like(pad)
    pad[0, :, RIM : RIM + rows, RIM : RIM + columns] = x_ref[...].astype(F32)
    pad[1, :, RIM : RIM + rows, RIM : RIM + columns] = g_ref[...].astype(F32)
    for t in range(frames):
        own[0, t] = jnp.zeros_like(own[0, t])
        own[0, t, :, :columns] = g_ref[t].astype(F32)

    starts = {-1: 0, 0: RIM}
    for k, direction in enumerate(DIRECTIONS):
        exists, there = places[k]
        r0 = starts.get(direction[0], RIM + rows)
        c0 = starts.get(direction[1], RIM + columns)
        _, nr, nc, _ = recv[k].shape

        @pl.when(exists)
        def _(k=k, there=there, r0=r0, c0=c0, nr=nr, nc=nc):
            copies[k].wait_send()
            pltpu.make_async_remote_copy(
                src_ref=stage[k],
                dst_ref=recv[k],
                send_sem=send_sem.at[k],
                recv_sem=recv_sem.at[k],
                device_id=there,
                device_id_type=MESH,
            ).wait_recv()
            value = recv[k][...].astype(F32)
            for which in range(2):
                pad[which, :, r0 : r0 + nr, c0 : c0 + nc] = value[
                    which * frames : (which + 1) * frames
                ]

    def inside(depth, wide, rim):
        shape = (depth, cols, chans)
        r = lax.broadcasted_iota(jnp.int32, shape, 0) + (me[0] * rows - rim)
        c = lax.broadcasted_iota(jnp.int32, shape, 1)
        place = c + (me[1] * columns - rim)
        ok = (r >= 0) & (r < rows * grid[0]) & (place >= 0) & (place < columns * grid[1])
        return ok & (c < wide)

    s1, h1, s2, h2 = s1_ref[...], h1_ref[...], s2_ref[...], h2_ref[...]
    ok1 = inside(deep, columns + 2 * RIM, RIM)
    for t in range(frames):
        z1 = pad[0, t] * s1 + h1
        store_wide(w1, t, jnp.where(ok1, z1 * sigmoid(z1), 0.0))
        store_wide(wg, t, pad[1, t])

    loads[0].wait()
    ok2 = inside(inner, columns + 2, 1)
    for t in range(frames):
        total = jnp.zeros((inner * cols, chans), F32)
        for kt in range(max(2 - t, 0), 3):
            for kw in range(3):
                weights = jnp.concatenate([k1_ref[kt, kh, kw] for kh in range(3)], axis=0)
                total = total + dot(
                    flat2(w1[t + kt - 2, kw : kw + inner]), weights, ((1,), (0,))
                )
        z2 = (total.reshape(inner, cols, chans) + b1_ref[...]) * s2 + h2
        sig = sigmoid(z2)
        store_wide(w2, t, jnp.where(ok2, z2 * sig, 0.0))
        ds2[t] = jnp.where(ok2, sig * (1.0 + z2 * (1.0 - sig)) * s2, 0.0)

    def put(which, at, value):
        size = terms.shape[1]
        end = at + value.shape[0]
        for k in range(GROUPS):
            low, high = max(at, k * size), min(end, (k + 1) * size)
            if low < high:
                terms[which * GROUPS + k, low - k * size : high - k * size] = value[
                    low - at : high - at
                ]

    def kernel_terms(which, wide, skip, grads):
        for kt in range(3):
            first = 2 - kt
            for kw in range(3):
                slab = wide[: frames - first, kw + skip : kw + skip + rows]
                term = dot(flat2(slab), flat2(grads[first:]), ((0,), (0,)))
                for kh in range(3):
                    at = (kt * 9 + kh * 3 + kw) * chans
                    put(which, at, term[kh * chans : (kh + 1) * chans])
        bias = jnp.sum(flat2(own[which]), axis=0, keepdims=True)
        tail = GROUPS * terms.shape[1] - taps
        lead = lax.broadcasted_iota(jnp.int32, (tail, chans), 0) == 0
        put(which, taps, jnp.where(lead, bias, 0.0))

    kernel_terms(0, w2, 0, own[0].astype(BF16))
    reducer.start(0)
    reducer.start(1)

    def back(wide, kernel_ref, t, depth):
        total = jnp.zeros((depth * cols, chans), F32)
        for kt in range(t, 3):
            for kw in range(3):
                weights = jnp.concatenate(
                    [kernel_ref[kt, 2 - kh, 2 - kw] for kh in range(3)], axis=1
                )
                total = total + dot(
                    flat2(wide[t + 2 - kt, kw : kw + depth]), weights, ((1,), (1,))
                )
        return total.reshape(depth, cols, chans)

    loads[1].wait()
    c = lax.broadcasted_iota(jnp.int32, (rows, cols, chans), 1)
    mine = (c >= 1) & (c <= columns)
    for t in range(frames):
        dc1 = (back(wg, k2_ref, t, inner) * ds2[t]).astype(BF16).astype(F32)
        store_wide(wd, t, dc1)
        own[1, t] = jnp.where(mine, dc1[1 : 1 + rows], 0.0)

    reducer.halves(0)
    reducer.halves(1)
    kernel_terms(1, w1, 1, own[1].astype(BF16))
    reducer.start(2)
    reducer.start(3)

    def input_grad(t):
        da1 = back(wd, k1_ref, t, rows)[:, :columns]
        z1 = x_ref[t].astype(F32) * s1 + h1
        sig = sigmoid(z1)
        slope = sig * (1.0 + z1 * (1.0 - sig))
        out_ref[t] = (g_ref[t].astype(F32) + da1 * slope * s1).astype(BF16)

    input_grad(0)
    reducer.halves(2)
    reducer.halves(3)
    reducer.parts(0)
    input_grad(1)
    reducer.parts(1)
    input_grad(2)
    reducer.pieces(0)
    reducer.pieces(1)
    reducer.parts(2)
    reducer.join_pieces(0)
    reducer.parts(3)
    reducer.join_pieces(1)
    reducer.pieces(2)
    reducer.pieces(3)
    reducer.join_parts(0)
    reducer.join_parts(1)
    reducer.join_pieces(2)
    reducer.join_pieces(3)
    reducer.join_parts(2)
    reducer.join_parts(3)
    for w in range(2 * GROUPS):
        reducer.finish(w)


def widen_kernel(taps, full, x_ref, two_ref, one_ref, bias_two_ref, bias_one_ref, y_ref):
    for w, (out_ref, bias_ref) in enumerate(((two_ref, bias_two_ref), (one_ref, bias_one_ref))):
        out_ref[...] = full[w, :taps].astype(F32)
        bias_ref[...] = full[w, taps : taps + 16].astype(F32)[0]
    y_ref[...] = x_ref[...]


def body(sizes, x, g, k1, b1, k2, s1, h1, s2, h2):
    x, g = (jnp.transpose(v, (0, 2, 1, 3)) for v in (x, g))
    frames, rows, columns, chans = x.shape
    factor = 1.0 / math.sqrt(frames * rows * sizes[1] * columns * sizes[0])
    taps = 27 * chans
    height = round_up(taps + 16, 8 * GROUPS * sizes[0] * sizes[1]) // GROUPS
    cols = round_up(columns + 2 * RIM, 16)
    deep, inner = rows + 2 * RIM, rows + 2
    many_b, many_c = 2 * sizes[0], sizes[1] // 4
    half = height // 2
    part = half // many_b
    piece = part // many_c
    many = 2 * GROUPS
    slots = [1, many_b - 1, many_c - 1, many_c - 1, many_b - 1, many_b]
    rims = [pltpu.VMEM(rim_shape(d, frames, rows, columns, chans), BF16) for d in DIRECTIONS]
    vectors = [v.reshape(1, chans) for v in (b1, s1, h1, s2, h2)]
    hbm = pl.BlockSpec(memory_space=pl.ANY)
    grad_input, full = pl.pallas_call(
        functools.partial(block_kernel, sizes, factor),
        name="block",
        out_shape=[
            jax.ShapeDtypeStruct(x.shape, BF16),
            jax.ShapeDtypeStruct((many, height, chans), BF16),
        ],
        in_specs=[VMEM, VMEM, hbm, VMEM, hbm] + [VMEM] * 4,
        out_specs=[VMEM] * 2,
        scratch_shapes=rims
        + rims
        + [pltpu.SemaphoreType.DMA((8,)), pltpu.SemaphoreType.DMA((8,))]
        + [pltpu.SemaphoreType.DMA((2,)), pltpu.VMEM(k1.shape, BF16), pltpu.VMEM(k2.shape, BF16)]
        + [
            pltpu.VMEM((2, frames, deep, cols, chans), F32),
            pltpu.VMEM((frames, deep, cols, 3 * chans), BF16),
            pltpu.VMEM((frames, deep, cols, 3 * chans), BF16),
            pltpu.VMEM((frames, inner, cols, 3 * chans), BF16),
            pltpu.VMEM((frames, inner, cols, 3 * chans), BF16),
            pltpu.VMEM((frames, inner, cols, chans), F32),
            pltpu.VMEM((2, frames, rows, cols, chans), F32),
            pltpu.VMEM((many, height, chans), F32),
        ]
        + [
            pltpu.VMEM((many, half, chans), BF16),
            pltpu.VMEM((many, half, chans), BF16),
            pltpu.VMEM((many, half, chans), BF16),
            pltpu.VMEM((many, many_b - 1, part, chans), BF16),
            pltpu.VMEM((many, part, chans), BF16),
            pltpu.VMEM((many, many_c - 1, piece, chans), BF16),
            pltpu.VMEM((many, half, chans), F32),
        ]
        + [pltpu.SemaphoreType.DMA((many, n)) for n in slots for _ in range(2)],
        compiler_params=pltpu.CompilerParams(collective_id=0, has_side_effects=True),
    )(x, g, k1, vectors[0], k2, *vectors[1:])
    grad_two, grad_one, bias_two, bias_one, grad_input = pl.pallas_call(
        functools.partial(widen_kernel, taps),
        name="widen",
        out_shape=[jax.ShapeDtypeStruct((taps, chans), F32)] * 2
        + [jax.ShapeDtypeStruct((chans,), F32)] * 2
        + [jax.ShapeDtypeStruct(x.shape, BF16)],
        in_specs=[VMEM] * 2,
        out_specs=[VMEM] * 5,
    )(full.reshape(2, GROUPS * height, chans), grad_input)
    return (
        jnp.transpose(grad_input, (0, 2, 1, 3)),
        grad_one.reshape(k1.shape),
        bias_one,
        grad_two.reshape(k2.shape),
        bias_two,
    )


def solution(mesh):
    sizes = (mesh.shape["ha"], mesh.shape["wa"])
    cells = P(None, "ha", "wa", None)
    return jax.shard_map(
        functools.partial(body, sizes),
        mesh=mesh,
        in_specs=(cells, cells) + (P(),) * 7,
        out_specs=(cells, P(), P(), P(), P()),
        check_vma=False,
    )
```
